512 devices in a mesh: task: 8 (over x_lo, y), shard: 64 (over z, x_hi, core).
Axes of the slice: x: 4 (x_hi: 2, x_lo: 2; x = x_hi * 2 + x_lo), y: 4, z: 16, core: 2. Of those that a mesh axis runs over, the one named last changes fastest.
Arguments:
- acts: bfloat16 [8, 1024, 4096], P('task', 'shard'), may hold values from -6 to 6
- cotangents: bfloat16 [8, 1024, 16384], P('task', 'shard'), may hold values from -0.75 to 0.75
- task_weights: bfloat16 [8, 4096, 16384], P('task', None, 'shard'), may hold values from -6 to 6
- example_count: int32 [8], P('task'), may hold values from 3 to 8, as said below
- example_start: int32 [8, 8], P('task'), may hold values from 0 to 1023, as said below
- example_len: int32 [8, 8], P('task'), may hold values from 1 to 128, as said below
Outputs:
- merged: bfloat16 [4096, 16384], P('task', 'shard')
The draws below stay inside these ranges and needn't reach their ends.
Inputs may be any that keep to these rules, and one draw needn't show every extreme that they name: Task t's examples are counted in slots 0 to example_count[t] - 1; some task has 8. Slot e of every task lies in rows e * 128 to (e + 1) * 128 - 1: example_start[t, e] >= e * 128 and example_start[t, e] + example_len[t, e] <= (e + 1) * 128. `example_len`: every task has a counted slot of exactly 128 rows.
All inputs are finite; a program needn't handle non-finite values.
Results may differ from the reference program's by a relative error of at most 0.007.
Values may be sent and summed in bfloat16 or wider, within the bound.
A program may use at most 128 MiB of HBM per device.

```python
import jax
import jax.numpy as jnp
from jax import lax

D = 4096
FF = 16384
EX = 8
MOST = 128
TASKS = 8
TOKENS = 1024


def example_table(key):
    base = jax.random.fold_in(key, 9173)
    key_count, key_len, key_start, key_top, key_long = jax.random.split(base, 5)
    lowest = (EX + 2) // 3
    count = jax.random.randint(key_count, (TASKS,), lowest, EX + 1)
    top_task = jax.random.randint(key_top, (), 0, TASKS)
    count = jnp.where(jnp.arange(TASKS) == top_task, EX, count).astype(jnp.int32)
    lengths = jax.random.randint(key_len, (TASKS, EX), 1, MOST + 1)
    long_slot = jax.random.randint(key_long, (TASKS,), 0, count)
    slots = jnp.arange(EX, dtype=jnp.int32)
    lengths = jnp.where(slots[None, :] == long_slot[:, None], MOST, lengths).astype(jnp.int32)
    offset = jax.random.randint(key_start, (TASKS, EX), 0, MOST + 1 - lengths)
    starts = (slots[None, :] * MOST + offset).astype(jnp.int32)
    return (count, starts, lengths)


def draw_example_count(key, part):
    return example_table(key)[0]


def draw_example_start(key, part):
    return example_table(key)[1]


def draw_example_len(key, part):
    return example_table(key)[2]


def steps_of(key, dims, cuts, low, top_value):
    gain, own = 1.0, jax.random.fold_in(key, 6)
    for axis_at, shards_of in cuts:
        draws = jnp.exp(jax.random.uniform(jax.random.fold_in(own, axis_at), (shards_of,), jnp.float32, low / len(cuts), top_value / len(cuts)))
        gain = gain * jnp.repeat(draws, dims[axis_at] // shards_of).reshape([-1 if axis == axis_at else 1 for axis in range(len(dims))])
    return gain


def bell_draw(own_key, shape, width, bound, pieces=(), kind=jnp.bfloat16):
    values = jax.random.normal(own_key, shape, jnp.float32) * width
    if len(pieces) > 0:
        values = steps_of(own_key, shape, pieces, -0.22, 0.18) * values
    return jnp.clip(values, min=-bound, max=bound).astype(kind)


def setup_inputs(seed: int = 0) -> dict:
    keys = jax.random.split(jax.random.key(seed), 7)
    acts = bell_draw(keys[0], (TASKS, TOKENS, D), 1.0, 6.0, ((0, 8), (1, 64)))
    cotangents = bell_draw(keys[1], (TASKS, TOKENS, FF), 0.125, 0.75, ((0, 8), (1, 64)))
    task_weights = bell_draw(keys[2], (TASKS, D, FF), 1.0, 6.0, ((0, 8), (2, 64)))
    example_count = draw_example_count(jax.random.fold_in(keys[6], 71), 0)
    example_start = draw_example_start(jax.random.fold_in(keys[6], 71), 0)
    example_len = draw_example_len(jax.random.fold_in(keys[6], 71), 0)
    return {"acts": acts, "cotangents": cotangents, "task_weights": task_weights, "example_count": example_count, "example_start": example_start, "example_len": example_len}


def task_fisher(rows, grads, count, starts, lengths):
    def one_slot(slot, total):
        block_x = lax.dynamic_slice_in_dim(rows, slot * MOST, MOST, 0)
        block_g = lax.dynamic_slice_in_dim(grads, slot * MOST, MOST, 0)
        position = slot * MOST + jnp.arange(MOST, dtype=jnp.int32)
        first = starts[slot]
        keep = (position >= first) & (position < first + lengths[slot]) & (slot < count)
        masked = jnp.where(keep[:, None], block_g, jnp.zeros_like(block_g))
        grad = jnp.dot(block_x.T, masked, preferred_element_type=jnp.float32)
        return total + grad * grad
    total = lax.fori_loop(0, EX, one_slot, jnp.zeros((D, FF), jnp.float32))
    return (total / count.astype(jnp.float32)).astype(jnp.bfloat16)


def reference(acts, cotangents, task_weights, example_count, example_start, example_len):
    numer = jnp.zeros((D, FF), jnp.float32)
    denom = jnp.zeros((D, FF), jnp.float32)
    for task in range(TASKS):
        fisher = task_fisher(acts[task], cotangents[task], example_count[task], example_start[task], example_len[task])
        weight_f = fisher.astype(jnp.float32)
        numer = numer + weight_f * task_weights[task].astype(jnp.float32)
        denom = denom + weight_f
    return (numer / (denom + 1e-6)).astype(jnp.bfloat16)
```

```python
import jax
import jax.numpy as jnp
from jax import lax
from jax.experimental import pallas as pl
from jax.experimental.pallas import tpu as pltpu
from jax.sharding import Mesh
from jax.sharding import PartitionSpec as P

XL, Y, Z, XH, C = 2, 4, 16, 2, 2
AXES = ("xl", "y", "z", "xh", "c")
EX = 8
MOST = 128
ROWS = 16
CHUNK = 256
NCH = 4
BLK = 256
DB = 512
TILE = 128
HALF = Z // 2


def kernel(count_ref, start_ref, len_ref, x_ref, g_ref, w_ref, o_ref,
           xs, gs, ws, fs, fr, mk,
           loc_sem, q_send, q_recv, r_send, r_recv,
           gz_send, gz_recv, gx_send, gx_recv, gc_send, gc_recv,
           w_send, w_recv, f_send, f_recv):
    xl, y, z, xh, c = (lax.axis_index(a) for a in AXES)
    task = xl * Y + y
    oxh, oc = 1 - xh, 1 - c
    quart = c * 2 + xh

    def zmod(v):
        return lax.rem(v + 2 * Z, Z)

    def remote(src, dst, ssem, rsem, **dev):
        return pltpu.make_async_remote_copy(
            src_ref=src, dst_ref=dst, send_sem=ssem, recv_sem=rsem,
            device_id=dev, device_id_type=pl.DeviceIdType.MESH)

    barrier = pltpu.get_barrier_semaphore()

    def tell(**dev):
        pl.semaphore_signal(barrier, inc=1, device_id=dev,
                            device_id_type=pl.DeviceIdType.MESH)

    tell(xh=xh, c=oc)
    tell(xh=oxh, c=c)
    tell(xh=oxh, c=oc)

    def tell_z(d, carry):
        tell(z=zmod(z + d))
        return carry
    lax.fori_loop(1, Z, tell_z, 0)

    def tell_t(k, carry):
        t2 = lax.rem(task + k, XL * Y)
        tell(xl=t2 // Y, y=lax.rem(t2, Y))
        return carry
    lax.fori_loop(1, XL * Y, tell_t, 0)

    src_q = task // 2
    src_c, src_xh = src_q // 2, lax.rem(src_q, 2)
    own_src = src_q == quart

    def tell_f(k, carry):
        t2 = lax.rem(task + k, XL * Y)
        tell(xl=t2 // Y, y=lax.rem(t2, Y), xh=src_xh, c=src_c)
        return carry
    lax.fori_loop(1, XL * Y, tell_f, 0)

    @pl.when(jnp.logical_not(own_src))
    def _():
        tell(xh=src_xh, c=src_c)

    me = xh * 2 + c

    def local_x(n):
        return pltpu.make_async_copy(
            x_ref.at[:, pl.ds(pl.multiple_of(quart * 1024 + n * CHUNK, 128), CHUNK)],
            xs.at[n, z, pl.ds(pl.multiple_of(me * ROWS, ROWS), ROWS), :], loc_sem.at[n])

    for n in range(NCH):
        local_x(n).start()
    own_g = g_ref.at[:, pl.ds(pl.multiple_of(z * 1024, 128), 1024)]
    local_g = pltpu.make_async_copy(own_g, gs.at[z, xh, c], loc_sem.at[4])
    local_g.start()
    local_w = pltpu.make_async_copy(
        w_ref.at[pl.ds(pl.multiple_of(task * DB, DB), DB), :], ws.at[task], loc_sem.at[5])
    local_w.start()

    position = lax.broadcasted_iota(jnp.int32, (MOST, 128), 0)
    for e in range(EX):
        first = start_ref[0, e] - e * MOST
        last = jnp.where(e < count_ref[0], first + len_ref[0, e], first)
        keep = jnp.where(position >= first, 1.0, 0.0) * jnp.where(position < last, 1.0, 0.0)
        mk[e] = keep.astype(jnp.bfloat16)

    pl.semaphore_wait(
        barrier, 3 + (Z - 1) + 2 * (XL * Y - 1) + 1 - own_src.astype(jnp.int32))

    def quad_copy(n, h, k):
        return remote(
            x_ref.at[:, pl.ds(pl.multiple_of((k * 2 + h) * 1024 + n * CHUNK, 128), CHUNK)],
            xs.at[n, z, pl.ds(pl.multiple_of(me * ROWS, ROWS), ROWS), :],
            q_send.at[n, h * 2 + k], q_recv.at[n, me], xh=h, c=k)

    def quad_arrival(n, h, k):
        return remote(
            x_ref.at[:, pl.ds(0, CHUNK)],
            xs.at[n, z, pl.ds(pl.multiple_of((h * 2 + k) * ROWS, ROWS), ROWS), :],
            q_send.at[n, me], q_recv.at[n, h * 2 + k], xh=h, c=k)

    others = ((oxh, c), (xh, oc), (oxh, oc))

    def order(m):
        return lax.rem(m // 2 + y, 2) * 2 + m % 2

    for m in range(NCH):
        for h, k in others:
            quad_copy(order(m), h, k).start()

    def gz_copy(zp):
        return remote(
            g_ref.at[:, pl.ds(pl.multiple_of(zp * 1024, 128), 1024)],
            gs.at[z, xh, c], gz_send.at[zp], gz_recv.at[z], z=zp)

    def gz_arrival(zp):
        return remote(own_g, gs.at[zp, xh, c], gz_send.at[z], gz_recv.at[zp], z=zp)

    gz_copy(zmod(z + HALF)).start()

    def far(i, carry):
        d = HALF - i
        gz_copy(zmod(z + d)).start()
        gz_copy(zmod(z - d)).start()
        return carry
    lax.fori_loop(1, HALF, far, 0)

    def w_copy(k):
        t2 = lax.rem(task + k, XL * Y)
        return remote(
            w_ref.at[pl.ds(pl.multiple_of(t2 * DB, DB), DB), :], ws.at[task],
            w_send.at[k], w_recv.at[k], xl=t2 // Y, y=lax.rem(t2, Y))

    def w_start(k, carry):
        w_copy(k).start()
        return carry
    lax.fori_loop(1, XL * Y, w_start, 0)

    def gx_copy(zp, src):
        return remote(src, gs.at[zp, xh, c], gx_send.at[zp], gx_recv.at[zp], xh=oxh)

    def gx_arrival(zp):
        return remote(own_g, gs.at[zp, oxh, c], gx_send.at[zp], gx_recv.at[zp], xh=oxh)

    def gc_copy(zp, h, src):
        return remote(src, gs.at[zp, h, c], gc_send.at[zp, h], gc_recv.at[zp, h], c=oc)

    def gc_arrival(zp, h):
        return remote(own_g, gs.at[zp, h, oc], gc_send.at[zp, h], gc_recv.at[zp, h], c=oc)

    def take_z(zp):
        gz_arrival(zp).wait_recv()
        gx_copy(zp, gs.at[zp, xh, c]).start()
        gc_copy(zp, xh, gs.at[zp, xh, c]).start()

    def take_x(zp):
        gx_arrival(zp).wait_recv()
        gc_copy(zp, oxh, gs.at[zp, oxh, c]).start()

    gx_copy(z, own_g).start()
    gc_copy(z, xh, own_g).start()

    def ring(way, s, m):
        n = order(m)
        step = 1 if way == 0 else -1
        held = zmod(z - step * (s - 1))
        return remote(xs.at[n, held], xs.at[n, held], r_send.at[way, m, s - 1],
                      r_recv.at[way, m, s - 1], z=zmod(z + step))

    def ring_arrival(way, s, m):
        n = order(m)
        step = 1 if way == 0 else -1
        came = zmod(z - step * s)
        return remote(xs.at[n, came], xs.at[n, came], r_send.at[way, m, s - 1],
                      r_recv.at[way, m, s - 1], z=zmod(z - step))

    for m in range(NCH):
        n = order(m)
        local_x(n).wait()
        for h, k in others:
            quad_arrival(n, h, k).wait_recv()
        ring(0, 1, m).start()
        ring(1, 1, m).start()

    def both(s, last):
        for m in range(NCH):
            for way in range(2):
                ring_arrival(way, s - 1, m).wait_recv()
                if not last or (m < 2) == (way == 0):
                    ring(way, s, m).start()

    both(2, False)
    take_x(z)

    def mid(s, carry):
        both(s, False)
        d = 11 - s
        take_z(zmod(z + d))

        @pl.when(d < HALF)
        def _():
            take_z(zmod(z - d))

        @pl.when(s > 3)
        def _():
            take_x(zmod(z + d + 1))

        @pl.when(s > 4)
        def _():
            take_x(zmod(z - d - 1))
        return carry
    lax.fori_loop(3, HALF, mid, 0)
    both(HALF, True)
    for d in (3, 2, 1):
        take_z(zmod(z + d))
        take_z(zmod(z - d))
        take_x(zmod(z + d + 1))
        take_x(zmod(z - d - 1))
    take_x(zmod(z + 1))
    take_x(zmod(z - 1))

    for m in range(NCH):
        ring_arrival(0 if m < 2 else 1, HALF, m).wait_recv()

    local_g.wait()

    def gc_wait(zp, carry):
        for h in range(2):
            gc_arrival(zp, h).wait_recv()
        return carry
    lax.fori_loop(0, Z, gc_wait, 0)

    inv = jnp.ones((1, BLK), jnp.float32) / jnp.full((1, BLK), count_ref[0].astype(jnp.float32))

    def tile_of(i):
        b = lax.rem(i // 4 + y, 2)
        return b, lax.rem(i, 4)

    def send_tile(i, act):
        b, r = tile_of(i)
        t2 = quart * 2 + b
        for f in range(4):
            h, k = f // 2, f % 2
            mine = jnp.logical_and(t2 == task, me == f)
            dst = fr.at[task, r]
            src = fs.at[i, f]

            @pl.when(jnp.logical_not(mine))
            def _():
                cp = remote(src, dst, f_send.at[i, f], f_recv.at[task, r],
                            xl=t2 // Y, y=lax.rem(t2, Y), xh=h, c=k)
                if act == "start":
                    cp.start()
                else:
                    cp.wait_send()

            @pl.when(mine)
            def _():
                if act == "start":
                    pltpu.make_async_copy(src, dst, f_recv.at[task, r]).start()

    def compute(i):
        b, r = tile_of(i)
        n = b * 2 + r // 2
        col = pl.multiple_of(lax.rem(r, 2) * TILE, TILE)
        xts = []
        for e in range(EX):
            xe = xs[n, 2 * e:2 * e + 2, :, pl.ds(col, TILE)].reshape(MOST, TILE) * mk[e]
            xts.append(xe.T)
        for f in range(4):
            total = jnp.zeros((TILE, BLK), jnp.float32)
            for e in range(EX):
                ge = gs[2 * e:2 * e + 2, :, :, :, f * BLK:(f + 1) * BLK].reshape(MOST, BLK)
                grad = jnp.dot(xts[e], ge, preferred_element_type=jnp.float32)
                total = total + grad * grad
            fs[i, f] = (total * inv).astype(jnp.bfloat16)

    def tile_step(i, carry):
        compute(i)

        @pl.when(i > 0)
        def _():
            send_tile(i - 1, "start")
        return carry
    lax.fori_loop(0, 8, tile_step, 0)
    send_tile(7, "start")

    local_w.wait()

    def w_wait(k, carry):
        w_copy(k).wait()
        return carry
    lax.fori_loop(1, XL * Y, w_wait, 0)

    def merge(r, carry):
        for t2 in range(XL * Y):
            pltpu.make_async_copy(fs.at[0, 0], fr.at[t2, r], f_recv.at[t2, r]).wait()
        rows = pl.ds(pl.multiple_of(r * TILE, TILE), TILE)
        numer = jnp.zeros((TILE, BLK), jnp.float32)
        denom = jnp.zeros((TILE, BLK), jnp.float32)
        for t2 in range(XL * Y):
            f32 = fr[t2, r].astype(jnp.float32)
            numer = numer + f32 * ws[t2, rows, :].astype(jnp.float32)
            denom = denom + f32
        o_ref[rows, :] = (numer / (denom + 1e-6)).astype(jnp.bfloat16)
        return carry
    lax.fori_loop(0, 4, merge, 0)

    for m in range(NCH):
        for h, k in others:
            quad_copy(order(m), h, k).wait_send()

    def z_out(d, carry):
        gz_copy(zmod(z + d)).wait_send()
        return carry
    lax.fori_loop(1, Z, z_out, 0)

    def q_out(zp, carry):
        gx_copy(zp, own_g).wait_send()
        gc_copy(zp, 0, own_g).wait_send()
        gc_copy(zp, 1, own_g).wait_send()
        return carry
    lax.fori_loop(0, Z, q_out, 0)

    def r_out(s, carry):
        for m in range(NCH):
            for way in range(2):
                ring(way, s, m).wait_send()
        return carry
    lax.fori_loop(1, HALF, r_out, 0)
    for m in range(NCH):
        ring(0 if m < 2 else 1, HALF, m).wait_send()

    def f_out(i, carry):
        send_tile(i, "wait")
        return carry
    lax.fori_loop(0, 8, f_out, 0)


def per_device(acts, cotangents, task_weights, example_count, example_start, example_len):
    dma = pltpu.SemaphoreType.DMA
    vmem = pltpu.VMEM
    bf = jnp.bfloat16
    return pl.pallas_call(
        kernel,
        out_shape=jax.ShapeDtypeStruct((DB, BLK), bf),
        in_specs=[pl.BlockSpec(memory_space=pltpu.SMEM)] * 3
        + [pl.BlockSpec(memory_space=pl.ANY)] * 3,
        out_specs=pl.BlockSpec(memory_space=pltpu.VMEM),
        scratch_shapes=[
            vmem((NCH, Z, 64, CHUNK), bf),
            vmem((Z, 2, 2, ROWS, 1024), bf),
            vmem((8, DB, BLK), bf),
            vmem((8, 4, TILE, BLK), bf),
            vmem((8, 4, TILE, BLK), bf),
            vmem((EX, MOST, 128), bf),
            dma((6,)),
            dma((NCH, 4)), dma((NCH, 4)),
            dma((2, NCH, HALF)), dma((2, NCH, HALF)),
            dma((Z,)), dma((Z,)),
            dma((Z,)), dma((Z,)),
            dma((Z, 2)), dma((Z, 2)),
            dma((8,)), dma((8,)),
            dma((8, 4)), dma((8, 4)),
        ],
        compiler_params=pltpu.CompilerParams(
            collective_id=0, has_side_effects=True, vmem_limit_bytes=40 << 20),
        name="merge",
    )(example_count, example_start, example_len,
      acts[0], cotangents[0], task_weights[0])


def solution(mesh):
    split = Mesh(mesh.devices.reshape(XL, Y, Z, XH, C), AXES)
    task, shard = ("xl", "y"), ("z", "xh", "c")
    in_specs = (
        P(task, shard, None),
        P(task, shard, None),
        P(task, None, shard),
        P(task),
        P(task, None),
        P(task, None),
    )
    return jax.shard_map(
        per_device, mesh=split, in_specs=in_specs, out_specs=P(task, shard), check_vma=False)
```

```python
import jax
import jax.numpy as jnp
from jax import lax
from jax.experimental import pallas as pl
from jax.experimental.pallas import tpu as pltpu
from jax.sharding import Mesh
from jax.sharding import PartitionSpec as P

XL, Y, Z, XH, C = 2, 4, 16, 2, 2
AXES = ("xl", "y", "z", "xh", "c")
EX = 8
MOST = 128
ROWS = 16
CHUNK = 256
NCH = 4
BLK = 256
DB = 512
TILE = 128
HALF = Z // 2
START = (1, 3, 5, 7)
FIRST = 11


def kernel(count_hbm, start_hbm, len_hbm, x_ref, g_ref, w_ref, o_ref,
           xs, gs, ws, fs, fr, mk, count_ref, start_ref, len_ref,
           cr, loc_sem, q_send, q_recv, r_send, r_recv,
           cz_send, cz_recv, gx_send, gx_recv, gc_send, gc_recv,
           w_send, w_recv, f_send, f_recv):
    xl, y, z, xh, c = (lax.axis_index(a) for a in AXES)
    task = xl * Y + y
    oxh, oc = 1 - xh, 1 - c
    quart = c * 2 + xh

    def zmod(v):
        return lax.rem(v + 2 * Z, Z)

    def remote(src, dst, ssem, rsem, **dev):
        return pltpu.make_async_remote_copy(
            src_ref=src, dst_ref=dst, send_sem=ssem, recv_sem=rsem,
            device_id=dev, device_id_type=pl.DeviceIdType.MESH)

    barrier = pltpu.get_barrier_semaphore()

    def tell(**dev):
        pl.semaphore_signal(barrier, inc=1, device_id=dev,
                            device_id_type=pl.DeviceIdType.MESH)

    tell(xh=xh, c=oc)
    tell(xh=oxh, c=c)
    tell(xh=oxh, c=oc)

    tell(z=zmod(z + 1))
    tell(z=zmod(z - 1))

    def tell_t(k, carry):
        t2 = lax.rem(task + k, XL * Y)
        tell(xl=t2 // Y, y=lax.rem(t2, Y))
        return carry
    lax.fori_loop(1, XL * Y, tell_t, 0)

    src_q = task // 2
    src_c, src_xh = src_q // 2, lax.rem(src_q, 2)
    own_src = src_q == quart

    def tell_f(k, carry):
        t2 = lax.rem(task + k, XL * Y)
        tell(xl=t2 // Y, y=lax.rem(t2, Y), xh=src_xh, c=src_c)
        return carry
    lax.fori_loop(1, XL * Y, tell_f, 0)

    @pl.when(jnp.logical_not(own_src))
    def _():
        tell(xh=src_xh, c=src_c)

    me = xh * 2 + c

    def local_x(n):
        return pltpu.make_async_copy(
            x_ref.at[:, pl.ds(pl.multiple_of(quart * 1024 + n * CHUNK, 128), CHUNK)],
            xs.at[n, z, pl.ds(pl.multiple_of(me * ROWS, ROWS), ROWS), :], loc_sem.at[n])

    for n in range(NCH):
        local_x(n).start()
    own_g = g_ref.at[:, pl.ds(pl.multiple_of(z * 1024, 128), 1024)]
    local_g = pltpu.make_async_copy(own_g, gs.at[z, xh, c], loc_sem.at[4])
    local_g.start()
    local_w = pltpu.make_async_copy(
        w_ref.at[pl.ds(pl.multiple_of(task * DB, DB), DB), :], ws.at[task], loc_sem.at[5])
    local_w.start()

    tables = [pltpu.make_async_copy(a, b, loc_sem.at[6 + i]) for i, (a, b) in enumerate(
        ((count_hbm, count_ref), (start_hbm, start_ref), (len_hbm, len_ref)))]
    for copy in tables:
        copy.start()
    for copy in tables:
        copy.wait()

    position = lax.broadcasted_iota(jnp.int32, (MOST, 128), 0)
    for e in range(EX):
        first = start_ref[0, e] - e * MOST
        last = jnp.where(e < count_ref[0], first + len_ref[0, e], first)
        keep = jnp.where(position >= first, 1.0, 0.0) * jnp.where(position < last, 1.0, 0.0)
        mk[e] = keep.astype(jnp.bfloat16)

    pl.semaphore_wait(
        barrier, 3 + 2 + 2 * (XL * Y - 1) + 1 - own_src.astype(jnp.int32))

    def quad_copy(n, h, k):
        return remote(
            x_ref.at[:, pl.ds(pl.multiple_of((k * 2 + h) * 1024 + n * CHUNK, 128), CHUNK)],
            xs.at[n, z, pl.ds(pl.multiple_of(me * ROWS, ROWS), ROWS), :],
            q_send.at[n, h * 2 + k], q_recv.at[n, me], xh=h, c=k)

    def quad_arrival(n, h, k):
        return remote(
            x_ref.at[:, pl.ds(0, CHUNK)],
            xs.at[n, z, pl.ds(pl.multiple_of((h * 2 + k) * ROWS, ROWS), ROWS), :],
            q_send.at[n, me], q_recv.at[n, h * 2 + k], xh=h, c=k)

    others = ((oxh, c), (xh, oc), (oxh, oc))

    def order(m):
        return lax.rem(m // 2 + y, 2) * 2 + m % 2

    for m in range(NCH):
        for h, k in others:
            quad_copy(order(m), h, k).start()

    def cols(way, dist, base):
        width = 512 if dist == HALF else 1024
        off = 512 if dist == HALF and way == 1 else 0
        return pl.ds(pl.multiple_of(base + off, 128), width)

    def cz(way, s, r, src, dst):
        return remote(src, dst, cz_send.at[way, s - 1, r], cz_recv.at[way, s - 1, r],
                      z=zmod(z + (1 if way == 0 else -1)))

    def cz_arrival(way, s, r, far):
        dst = cr.at[way, 0, 0, :, cols(way, HALF if far else 0, 0)]
        cz(way, s, r, dst, dst).wait_recv()

    def cz_first(way, r):
        far = r + 1 == HALF
        dest = zmod(z + (r + 1) * (1 if way == 0 else -1))
        src = g_ref.at[:, cols(way, r + 1, dest * 1024)]
        if r == 0:
            dst = gs.at[z, xh, c]
        else:
            dst = cr.at[way, 0, r - 1, :, cols(way, r + 1, 0)]
        cz(way, 1, r, src, dst).start()

    def cz_pass(way, s, r, far, final):
        cz_arrival(way, s - 1, r + 1, far)
        dist = HALF if far else 0
        src = cr.at[way, s - 2, r, :, cols(way, dist, 0)]
        if final:
            origin = zmod(z - (s - 1) * (1 if way == 0 else -1))
            dst = gs.at[origin, xh, c, :, cols(way, dist, 0)]
        else:
            dst = cr.at[way, s - 1, r - 1, :, cols(way, dist, 0)]
        cz(way, s, r, src, dst).start()

    def cz_step(s):
        @pl.when(s < HALF)
        def _():
            for way in range(2):
                cz_pass(way, s, HALF - s, True, False)

            def middle(j, carry):
                for way in range(2):
                    cz_pass(way, s, HALF - 1 - s - j, False, False)
                return carry
            lax.fori_loop(0, HALF - 1 - s, middle, 0)
            for way in range(2):
                cz_pass(way, s, 0, False, True)

        @pl.when(s == HALF)
        def _():
            for way in range(2):
                cz_pass(way, s, 0, True, True)

    def cz_wait_send(way, s, r, far):
        src = cr.at[way, 0, 0, :, cols(way, HALF if far else 0, 0)]
        cz(way, s, r, src, src).wait_send()

    def w_copy(k, piece=None):
        t2 = lax.rem(task + k, XL * Y)
        if piece is None:
            base, rows, span = t2 * DB, pl.ds(0, DB), DB
        else:
            base, rows, span = t2 * DB + piece * 64, pl.ds(pl.multiple_of(piece * 64, 64), 64), 64
        return remote(
            w_ref.at[pl.ds(pl.multiple_of(base, 64), span), :], ws.at[task, rows, :],
            w_send.at[k], w_recv.at[k], xl=t2 // Y, y=lax.rem(t2, Y))

    def w_some(piece):
        def one(k, carry):
            w_copy(k, piece).start()
            return carry
        lax.fori_loop(1, XL * Y, one, 0)

    def gx_copy(zp, src):
        return remote(src, gs.at[zp, xh, c], gx_send.at[zp], gx_recv.at[zp], xh=oxh)

    def gx_arrival(zp):
        return remote(own_g, gs.at[zp, oxh, c], gx_send.at[zp], gx_recv.at[zp], xh=oxh)

    def gc_copy(zp, h, src):
        return remote(src, gs.at[zp, h, c], gc_send.at[zp, h], gc_recv.at[zp, h], c=oc)

    def gc_arrival(zp, h):
        return remote(own_g, gs.at[zp, h, oc], gc_send.at[zp, h], gc_recv.at[zp, h], c=oc)

    def pass_on(zp):
        gx_copy(zp, gs.at[zp, xh, c]).start()
        gc_copy(zp, xh, gs.at[zp, xh, c]).start()

    def take_z(s):
        @pl.when(s < HALF)
        def _():
            for way in range(2):
                cz_arrival(way, s, 0, False)
                pass_on(zmod(z - s * (1 if way == 0 else -1)))

        @pl.when(s == HALF)
        def _():
            for way in range(2):
                cz_arrival(way, s, 0, True)
            pass_on(zmod(z + HALF))

    def take_x(zp):
        gx_arrival(zp).wait_recv()
        gc_copy(zp, oxh, gs.at[zp, oxh, c]).start()

    gx_copy(z, own_g).start()
    gc_copy(z, xh, own_g).start()

    for r in range(HALF - 1, -1, -1):
        for way in range(2):
            cz_first(way, r)

    def ring(way, s, m):
        n = order(m)
        step = 1 if way == 0 else -1
        held = zmod(z - step * (s - 1))
        return remote(xs.at[n, held], xs.at[n, held], r_send.at[way, m, s - 1],
                      r_recv.at[way, m, s - 1], z=zmod(z + step))

    def ring_arrival(way, s, m):
        n = order(m)
        step = 1 if way == 0 else -1
        came = zmod(z - step * s)
        return remote(xs.at[n, came], xs.at[n, came], r_send.at[way, m, s - 1],
                      r_recv.at[way, m, s - 1], z=zmod(z - step))

    def ring_part(slot, m):
        s = slot - START[m]

        @pl.when(s == 1)
        def _():
            n = order(m)
            local_x(n).wait()
            for h, k in others:
                quad_arrival(n, h, k).wait_recv()

        for way in range(2):
            turns = HALF if (m < 2) == (way == 0) else HALF - 1

            @pl.when(jnp.logical_and(s >= 2, s <= turns + 1))
            def _():
                ring_arrival(way, s - 1, m).wait_recv()

            @pl.when(jnp.logical_and(s >= 1, s <= turns))
            def _():
                ring(way, s, m).start()

    def take_pair(d, fn):
        fn(zmod(z + d))

        @pl.when(d < HALF)
        def _():
            fn(zmod(z - d))

    def early(slot, carry):
        @pl.when(jnp.logical_and(slot >= 2, slot <= HALF))
        def _():
            cz_step(slot)
        for m in range(NCH):
            ring_part(slot, m)

        @pl.when(jnp.logical_and(slot >= 2, slot <= HALF + 1))
        def _():
            take_z(slot - 1)

        @pl.when(jnp.logical_and(slot >= 3, slot <= HALF + 2))
        def _():
            take_pair(slot - 2, take_x)

        @pl.when(slot == 1)
        def _():
            take_x(z)

        @pl.when(slot <= 8)
        def _():
            w_some(slot - 1)
        return carry

    lax.fori_loop(1, FIRST, early, 0)
    local_g.wait()

    def gc_wait(zp, carry):
        for h in range(2):
            gc_arrival(zp, h).wait_recv()
        return carry
    lax.fori_loop(0, Z, gc_wait, 0)

    inv = jnp.ones((1, BLK), jnp.float32) / jnp.full((1, BLK), count_ref[0].astype(jnp.float32))

    def tile_of(i):
        b = lax.rem(i // 4 + y, 2)
        return b, lax.rem(i, 4)

    def send_part(i, f, act):
        b, r = tile_of(i)
        t2 = quart * 2 + b
        h, k = f // 2, f % 2
        mine = jnp.logical_and(t2 == task, me == f)
        dst = fr.at[task, r]
        src = fs.at[i, f]

        @pl.when(jnp.logical_not(mine))
        def _():
            cp = remote(src, dst, f_send.at[i, f], f_recv.at[task, r],
                        xl=t2 // Y, y=lax.rem(t2, Y), xh=h, c=k)
            if act == "start":
                cp.start()
            else:
                cp.wait_send()

        if act == "start":
            @pl.when(mine)
            def _():
                pltpu.make_async_copy(src, dst, f_recv.at[task, r]).start()

    def compute(i):
        b, r = tile_of(i)
        n = b * 2 + r // 2
        col = pl.multiple_of(lax.rem(r, 2) * TILE, TILE)
        xts = []
        for e in range(EX):
            xe = xs[n, 2 * e:2 * e + 2, :, pl.ds(col, TILE)].reshape(MOST, TILE) * mk[e]
            xts.append(xe.T)
        for f in range(4):
            total = jnp.zeros((TILE, BLK), jnp.float32)
            for e in range(EX):
                ge = gs[2 * e:2 * e + 2, :, :, :, f * BLK:(f + 1) * BLK].reshape(MOST, BLK)
                grad = jnp.dot(xts[e], ge, preferred_element_type=jnp.float32)
                total = total + grad * grad
            fs[i, f] = (total * inv).astype(jnp.bfloat16)
            if f > 0:
                send_part(i, f - 1, "start")

    def tile_step(i, carry):
        for m in range(NCH):
            ring_part(i + FIRST, m)

        @pl.when(i > 0)
        def _():
            send_part(i - 1, 3, "start")
        compute(i)
        return carry
    lax.fori_loop(0, 8, tile_step, 0)
    send_part(7, 3, "start")

    local_w.wait()

    def w_wait(k, carry):
        w_copy(k).wait()
        return carry
    lax.fori_loop(1, XL * Y, w_wait, 0)

    def merge(r, carry):
        for t2 in range(XL * Y):
            pltpu.make_async_copy(fs.at[0, 0], fr.at[t2, r], f_recv.at[t2, r]).wait()
        rows = pl.ds(pl.multiple_of(r * TILE, TILE), TILE)
        numer = jnp.zeros((TILE, BLK), jnp.float32)
        denom = jnp.zeros((TILE, BLK), jnp.float32)
        for t2 in range(XL * Y):
            f32 = fr[t2, r].astype(jnp.float32)
            numer = numer + f32 * ws[t2, rows, :].astype(jnp.float32)
            denom = denom + f32
        o_ref[rows, :] = (numer / (denom + 1e-6)).astype(jnp.bfloat16)
        return carry
    lax.fori_loop(0, 4, merge, 0)

    for m in range(NCH):
        for h, k in others:
            quad_copy(order(m), h, k).wait_send()

    def c_out(s, carry):
        for way in range(2):
            cz_wait_send(way, s, HALF - s, True)

        def near(r, carry):
            for way in range(2):
                cz_wait_send(way, s, r, False)
            return carry
        return lax.fori_loop(0, HALF - s, near, carry)
    lax.fori_loop(1, HALF + 1, c_out, 0)

    def q_out(zp, carry):
        gx_copy(zp, own_g).wait_send()
        gc_copy(zp, 0, own_g).wait_send()
        gc_copy(zp, 1, own_g).wait_send()
        return carry
    lax.fori_loop(0, Z, q_out, 0)

    def r_out(s, carry):
        for m in range(NCH):
            for way in range(2):
                ring(way, s, m).wait_send()
        return carry
    lax.fori_loop(1, HALF, r_out, 0)
    for m in range(NCH):
        ring(0 if m < 2 else 1, HALF, m).wait_send()

    def f_out(i, carry):
        for f in range(4):
            send_part(i, f, "wait")
        return carry
    lax.fori_loop(0, 8, f_out, 0)


def per_device(acts, cotangents, task_weights, example_count, example_start, example_len):
    dma = pltpu.SemaphoreType.DMA
    vmem = pltpu.VMEM
    bf = jnp.bfloat16
    return pl.pallas_call(
        kernel,
        out_shape=jax.ShapeDtypeStruct((DB, BLK), bf),
        in_specs=[pl.BlockSpec(memory_space=pl.ANY)] * 6,
        out_specs=pl.BlockSpec(memory_space=pltpu.VMEM),
        scratch_shapes=[
            vmem((NCH, Z, 64, CHUNK), bf),
            vmem((Z, 2, 2, ROWS, 1024), bf),
            vmem((8, DB, BLK), bf),
            vmem((8, 4, TILE, BLK), bf),
            vmem((8, 4, TILE, BLK), bf),
            vmem((EX, MOST, 128), bf),
            pltpu.SMEM((1,), jnp.int32), pltpu.SMEM((1, EX), jnp.int32),
            pltpu.SMEM((1, EX), jnp.int32),
            vmem((2, HALF - 1, HALF - 1, ROWS, 1024), bf), dma((9,)),
            dma((NCH, 4)), dma((NCH, 4)),
            dma((2, NCH, HALF)), dma((2, NCH, HALF)),
            dma((2, HALF, HALF)), dma((2, HALF, HALF)),
            dma((Z,)), dma((Z,)),
            dma((Z, 2)), dma((Z, 2)),
            dma((8,)), dma((8,)),
            dma((8, 4)), dma((8, 4)),
        ],
        compiler_params=pltpu.CompilerParams(
            collective_id=0, has_side_effects=True, vmem_limit_bytes=67_000_000),
        name="merge",
    )(example_count, example_start, example_len,
      acts[0], cotangents[0], task_weights[0])


def solution(mesh):
    split = Mesh(mesh.devices.reshape(XL, Y, Z, XH, C), AXES)
    task, shard = ("xl", "y"), ("z", "xh", "c")
    in_specs = (
        P(task, shard, None),
        P(task, shard, None),
        P(task, None, shard),
        P(task),
        P(task, None),
        P(task, None),
    )
    return jax.shard_map(
        per_device, mesh=split, in_specs=in_specs, out_specs=P(task, shard), check_vma=False)
```

```python
import jax
import jax.numpy as jnp
from jax import lax
from jax.experimental import pallas as pl
from jax.experimental.pallas import tpu as pltpu
from jax.sharding import Mesh
from jax.sharding import PartitionSpec as P

XL, Y, Z, XH, C = 2, 4, 16, 2, 2
AXES = ("xl", "y", "z", "xh", "c")
EX = 8
MOST = 128
ROWS = 16
CHUNK = 256
NCH = 4
BLK = 256
DB = 512
TILE = 128
HALF = Z // 2
START = (1, 3, 5, 7)
FIRST = 10
PIECES = (1, 1, 1, 1, 1, 1, 1, 1)


def kernel(count_hbm, start_hbm, len_hbm, x_ref, g_ref, w_ref, o_ref,
           xs, gs, ws, fs, fr, mk, count_ref, start_ref, len_ref,
           cr, loc_sem, q_send, q_recv, r_send, r_recv,
           cz_send, cz_recv, gx_send, gx_recv, gc_send, gc_recv,
           w_send, w_recv, f_send, f_recv):
    xl, y, z, xh, c = (lax.axis_index(a) for a in AXES)
    task = xl * Y + y
    oxh, oc = 1 - xh, 1 - c
    quart = c * 2 + xh

    def zmod(v):
        return lax.rem(v + 2 * Z, Z)

    def remote(src, dst, ssem, rsem, **dev):
        return pltpu.make_async_remote_copy(
            src_ref=src, dst_ref=dst, send_sem=ssem, recv_sem=rsem,
            device_id=dev, device_id_type=pl.DeviceIdType.MESH)

    barrier = pltpu.get_barrier_semaphore()

    def tell(**dev):
        pl.semaphore_signal(barrier, inc=1, device_id=dev,
                            device_id_type=pl.DeviceIdType.MESH)

    tell(xh=xh, c=oc)
    tell(xh=oxh, c=c)
    tell(xh=oxh, c=oc)

    tell(z=zmod(z + 1))
    tell(z=zmod(z - 1))

    def tell_t(k, carry):
        t2 = lax.rem(task + k, XL * Y)
        tell(xl=t2 // Y, y=lax.rem(t2, Y))
        return carry
    lax.fori_loop(1, XL * Y, tell_t, 0)

    src_q = task // 2
    src_c, src_xh = src_q // 2, lax.rem(src_q, 2)
    own_src = src_q == quart

    def tell_f(k, carry):
        t2 = lax.rem(task + k, XL * Y)
        tell(xl=t2 // Y, y=lax.rem(t2, Y), xh=src_xh, c=src_c)
        return carry
    lax.fori_loop(1, XL * Y, tell_f, 0)

    @pl.when(jnp.logical_not(own_src))
    def _():
        tell(xh=src_xh, c=src_c)

    me = xh * 2 + c

    def local_x(n):
        return pltpu.make_async_copy(
            x_ref.at[:, pl.ds(pl.multiple_of(quart * 1024 + n * CHUNK, 128), CHUNK)],
            xs.at[n, z, pl.ds(pl.multiple_of(me * ROWS, ROWS), ROWS), :], loc_sem.at[n])

    for n in range(NCH):
        local_x(n).start()
    own_g = g_ref.at[:, pl.ds(pl.multiple_of(z * 1024, 128), 1024)]
    local_g = pltpu.make_async_copy(own_g, gs.at[z, xh, c], loc_sem.at[4])
    local_g.start()
    local_w = pltpu.make_async_copy(
        w_ref.at[pl.ds(pl.multiple_of(task * DB, DB), DB), :], ws.at[task], loc_sem.at[5])
    local_w.start()

    tables = [pltpu.make_async_copy(a, b, loc_sem.at[6 + i]) for i, (a, b) in enumerate(
        ((count_hbm, count_ref), (start_hbm, start_ref), (len_hbm, len_ref)))]
    for copy in tables:
        copy.start()
    for copy in tables:
        copy.wait()

    position = lax.broadcasted_iota(jnp.int32, (MOST, 128), 0)
    for e in range(EX):
        first = start_ref[0, e] - e * MOST
        last = jnp.where(e < count_ref[0], first + len_ref[0, e], first)
        keep = jnp.where(position >= first, 1.0, 0.0) * jnp.where(position < last, 1.0, 0.0)
        mk[e] = keep.astype(jnp.bfloat16)

    pl.semaphore_wait(
        barrier, 3 + 2 + 2 * (XL * Y - 1) + 1 - own_src.astype(jnp.int32))

    def quad_copy(n, h, k):
        return remote(
            x_ref.at[:, pl.ds(pl.multiple_of((k * 2 + h) * 1024 + n * CHUNK, 128), CHUNK)],
            xs.at[n, z, pl.ds(pl.multiple_of(me * ROWS, ROWS), ROWS), :],
            q_send.at[n, h * 2 + k], q_recv.at[n, me], xh=h, c=k)

    def quad_arrival(n, h, k):
        return remote(
            x_ref.at[:, pl.ds(0, CHUNK)],
            xs.at[n, z, pl.ds(pl.multiple_of((h * 2 + k) * ROWS, ROWS), ROWS), :],
            q_send.at[n, me], q_recv.at[n, h * 2 + k], xh=h, c=k)

    others = ((oxh, c), (xh, oc), (oxh, oc))

    def order(m):
        return lax.rem(m + y, 2) * 2 + m // 2

    for m in range(NCH):
        for h, k in others:
            quad_copy(order(m), h, k).start()

    def cols(way, dist, base):
        width = 512 if dist == HALF else 1024
        off = 512 if dist == HALF and way == 1 else 0
        return pl.ds(pl.multiple_of(base + off, 128), width)

    def cz(way, s, r, src, dst):
        return remote(src, dst, cz_send.at[way, s - 1, r], cz_recv.at[way, s - 1, r],
                      z=zmod(z + (1 if way == 0 else -1)))

    def cz_arrival(way, s, r, far):
        dst = cr.at[way, 0, 0, :, cols(way, HALF if far else 0, 0)]
        cz(way, s, r, dst, dst).wait_recv()

    def cz_first(way, r):
        far = r + 1 == HALF
        dest = zmod(z + (r + 1) * (1 if way == 0 else -1))
        src = g_ref.at[:, cols(way, r + 1, dest * 1024)]
        if r == 0:
            dst = gs.at[z, xh, c]
        else:
            dst = cr.at[way, 0, r - 1, :, cols(way, r + 1, 0)]
        cz(way, 1, r, src, dst).start()

    def cz_pass(way, s, r, far, final):
        cz_arrival(way, s - 1, r + 1, far)
        dist = HALF if far else 0
        src = cr.at[way, s - 2, r, :, cols(way, dist, 0)]
        if final:
            origin = zmod(z - (s - 1) * (1 if way == 0 else -1))
            dst = gs.at[origin, xh, c, :, cols(way, dist, 0)]
        else:
            dst = cr.at[way, s - 1, r - 1, :, cols(way, dist, 0)]
        cz(way, s, r, src, dst).start()

    def cz_step(s):
        @pl.when(s < HALF)
        def _():
            for way in range(2):
                cz_pass(way, s, HALF - s, True, False)

            def middle(j, carry):
                for way in range(2):
                    cz_pass(way, s, HALF - 1 - s - j, False, False)
                return carry
            lax.fori_loop(0, HALF - 1 - s, middle, 0)
            for way in range(2):
                cz_pass(way, s, 0, False, True)

        @pl.when(s == HALF)
        def _():
            for way in range(2):
                cz_pass(way, s, 0, True, True)

    def cz_wait_send(way, s, r, far):
        src = cr.at[way, 0, 0, :, cols(way, HALF if far else 0, 0)]
        cz(way, s, r, src, src).wait_send()

    def w_copy(k, piece=None):
        t2 = lax.rem(task + k, XL * Y)
        if piece is None:
            base, rows, span = t2 * DB, pl.ds(0, DB), DB
        else:
            base, rows, span = t2 * DB + piece * 64, pl.ds(pl.multiple_of(piece * 64, 64), 64), 64
        return remote(
            w_ref.at[pl.ds(pl.multiple_of(base, 64), span), :], ws.at[task, rows, :],
            w_send.at[k], w_recv.at[k], xl=t2 // Y, y=lax.rem(t2, Y))

    def w_some(piece):
        def one(k, carry):
            w_copy(k, piece).start()
            return carry
        lax.fori_loop(1, XL * Y, one, 0)

    def gx_copy(zp, src):
        return remote(src, gs.at[zp, xh, c], gx_send.at[zp], gx_recv.at[zp], xh=oxh)

    def gx_arrival(zp):
        return remote(own_g, gs.at[zp, oxh, c], gx_send.at[zp], gx_recv.at[zp], xh=oxh)

    def gc_copy(zp, h, src):
        return remote(src, gs.at[zp, h, c], gc_send.at[zp, h], gc_recv.at[0], c=oc)

    def gc_all():
        whole = gs.at[:, :, oc]
        pltpu.make_async_copy(whole, whole, gc_recv.at[0]).wait()

    def pass_on(zp):
        gx_copy(zp, gs.at[zp, xh, c]).start()
        gc_copy(zp, xh, gs.at[zp, xh, c]).start()

    def take_z(s):
        @pl.when(s < HALF)
        def _():
            for way in range(2):
                cz_arrival(way, s, 0, False)
                pass_on(zmod(z - s * (1 if way == 0 else -1)))

        @pl.when(s == HALF)
        def _():
            for way in range(2):
                cz_arrival(way, s, 0, True)
            pass_on(zmod(z + HALF))

    def take_x(zp):
        gx_arrival(zp).wait_recv()
        gc_copy(zp, oxh, gs.at[zp, oxh, c]).start()

    gx_copy(z, own_g).start()
    gc_copy(z, xh, own_g).start()

    for r in range(HALF - 1, -1, -1):
        for way in range(2):
            cz_first(way, r)

    def ring(way, s, m):
        n = order(m)
        step = 1 if way == 0 else -1
        held = zmod(z - step * (s - 1))
        return remote(xs.at[n, held], xs.at[n, held], r_send.at[way, m, s - 1],
                      r_recv.at[way, m, s - 1], z=zmod(z + step))

    def ring_arrival(way, s, m):
        n = order(m)
        step = 1 if way == 0 else -1
        came = zmod(z - step * s)
        return remote(xs.at[n, came], xs.at[n, came], r_send.at[way, m, s - 1],
                      r_recv.at[way, m, s - 1], z=zmod(z - step))

    def ring_part(slot, m):
        s = slot - START[m]

        @pl.when(s == 1)
        def _():
            n = order(m)
            local_x(n).wait()
            for h, k in others:
                quad_arrival(n, h, k).wait_recv()

        for way in range(2):
            turns = HALF if (m < 2) == (way == 0) else HALF - 1

            @pl.when(jnp.logical_and(s >= 2, s <= turns + 1))
            def _():
                ring_arrival(way, s - 1, m).wait_recv()

            @pl.when(jnp.logical_and(s >= 1, s <= turns))
            def _():
                ring(way, s, m).start()

    def take_pair(d, fn):
        fn(zmod(z + d))

        @pl.when(d < HALF)
        def _():
            fn(zmod(z - d))

    def early(slot, carry):
        @pl.when(jnp.logical_and(slot >= 2, slot <= HALF))
        def _():
            cz_step(slot)

        @pl.when(slot >= 2)
        def _():
            take_z(slot - 1)

        @pl.when(slot >= 4)
        def _():
            take_pair(slot - 3, take_x)

        @pl.when(slot == 2)
        def _():
            take_x(z)
        for m in range(NCH):
            ring_part(slot, m)
        sent = 0
        for at, n in enumerate(PIECES):
            if n:
                @pl.when(slot == at)
                def _(lo=sent, hi=sent + n):
                    for piece in range(lo, hi):
                        w_some(piece)
            sent += n
        return carry

    for piece in range(PIECES[0]):
        w_some(piece)
    lax.fori_loop(1, FIRST, early, 0)
    take_pair(FIRST - 3, take_x)
    take_pair(FIRST - 2, take_x)
    local_g.wait()

    gc_all()

    inv = jnp.ones((1, BLK), jnp.float32) / jnp.full((1, BLK), count_ref[0].astype(jnp.float32))

    def tile_of(i):
        b = lax.rem(i // 2 + y, 2)
        return b, (i // 4) * 2 + lax.rem(i, 2)

    def send_part(i, f, act):
        b, r = tile_of(i)
        t2 = quart * 2 + b
        h, k = f // 2, f % 2
        mine = jnp.logical_and(t2 == task, me == f)
        dst = fr.at[task, r]
        src = fs.at[i, f]

        @pl.when(jnp.logical_not(mine))
        def _():
            cp = remote(src, dst, f_send.at[i, f], f_recv.at[task, r],
                        xl=t2 // Y, y=lax.rem(t2, Y), xh=h, c=k)
            if act == "start":
                cp.start()
            else:
                cp.wait_send()

        if act == "start":
            @pl.when(mine)
            def _():
                pltpu.make_async_copy(src, dst, f_recv.at[task, r]).start()

    def compute(i):
        b, r = tile_of(i)
        n = b * 2 + r // 2
        col = pl.multiple_of(lax.rem(r, 2) * TILE, TILE)
        xts = []
        for e in range(EX):
            xe = xs[n, 2 * e:2 * e + 2, :, pl.ds(col, TILE)].reshape(MOST, TILE) * mk[e]
            xts.append(xe.T)
        for f in range(4):
            total = jnp.zeros((TILE, BLK), jnp.float32)
            for e in range(EX):
                ge = gs[2 * e:2 * e + 2, :, :, :, f * BLK:(f + 1) * BLK].reshape(MOST, BLK)
                grad = jnp.dot(xts[e], ge, preferred_element_type=jnp.float32)
                total = total + grad * grad
            fs[i, f] = (total * inv).astype(jnp.bfloat16)
            if f > 0:
                send_part(i, f - 1, "start")

    def tile_step(i, carry):
        for m in range(NCH):
            ring_part(i + FIRST, m)

        @pl.when(i > 0)
        def _():
            send_part(i - 1, 3, "start")
        compute(i)
        return carry
    lax.fori_loop(0, 8, tile_step, 0)
    send_part(7, 3, "start")

    local_w.wait()

    def w_wait(k, carry):
        w_copy(k).wait()
        return carry
    lax.fori_loop(1, XL * Y, w_wait, 0)

    for m in range(NCH):
        for h, k in others:
            quad_copy(order(m), h, k).wait_send()

    def c_out(s, carry):
        for way in range(2):
            cz_wait_send(way, s, HALF - s, True)

        def near(r, carry):
            for way in range(2):
                cz_wait_send(way, s, r, False)
            return carry
        return lax.fori_loop(0, HALF - s, near, carry)
    lax.fori_loop(1, HALF + 1, c_out, 0)

    def q_out(zp, carry):
        gx_copy(zp, own_g).wait_send()
        gc_copy(zp, 0, own_g).wait_send()
        gc_copy(zp, 1, own_g).wait_send()
        return carry
    lax.fori_loop(0, Z, q_out, 0)

    def r_out(s, carry):
        for m in range(NCH):
            for way in range(2):
                ring(way, s, m).wait_send()
        return carry
    lax.fori_loop(1, HALF, r_out, 0)
    for m in range(NCH):
        ring(0 if m < 2 else 1, HALF, m).wait_send()

    def f_out(i, carry):
        for f in range(4):
            send_part(i, f, "wait")
        return carry
    lax.fori_loop(0, 8, f_out, 0)

    def merge(r, carry):
        for t2 in range(XL * Y):
            pltpu.make_async_copy(fs.at[0, 0], fr.at[t2, r], f_recv.at[t2, r]).wait()
        rows = pl.ds(pl.multiple_of(r * TILE, TILE), TILE)
        numer = jnp.zeros((TILE, BLK), jnp.float32)
        denom = jnp.zeros((TILE, BLK), jnp.float32)
        for t2 in range(XL * Y):
            f32 = fr[t2, r].astype(jnp.float32)
            numer = numer + f32 * ws[t2, rows, :].astype(jnp.float32)
            denom = denom + f32
        o_ref[rows, :] = (numer / (denom + 1e-6)).astype(jnp.bfloat16)
        return carry
    lax.fori_loop(0, 4, merge, 0)


def per_device(acts, cotangents, task_weights, example_count, example_start, example_len):
    dma = pltpu.SemaphoreType.DMA
    vmem = pltpu.VMEM
    bf = jnp.bfloat16
    return pl.pallas_call(
        kernel,
        out_shape=jax.ShapeDtypeStruct((DB, BLK), bf),
        in_specs=[pl.BlockSpec(memory_space=pl.ANY)] * 6,
        out_specs=pl.BlockSpec(memory_space=pltpu.VMEM),
        scratch_shapes=[
            vmem((NCH, Z, 64, CHUNK), bf),
            vmem((Z, 2, 2, ROWS, 1024), bf),
            vmem((8, DB, BLK), bf),
            vmem((8, 4, TILE, BLK), bf),
            vmem((8, 4, TILE, BLK), bf),
            vmem((EX, MOST, 128), bf),
            pltpu.SMEM((1,), jnp.int32), pltpu.SMEM((1, EX), jnp.int32),
            pltpu.SMEM((1, EX), jnp.int32),
            vmem((2, HALF - 1, HALF - 1, ROWS, 1024), bf), dma((9,)),
            dma((NCH, 4)), dma((NCH, 4)),
            dma((2, NCH, HALF)), dma((2, NCH, HALF)),
            dma((2, HALF, HALF)), dma((2, HALF, HALF)),
            dma((Z,)), dma((Z,)),
            dma((Z, 2)), dma((1,)),
            dma((8,)), dma((8,)),
            dma((8, 4)), dma((8, 4)),
        ],
        compiler_params=pltpu.CompilerParams(
            collective_id=0, has_side_effects=True, vmem_limit_bytes=67_000_000),
        name="merge",
    )(example_count, example_start, example_len,
      acts[0], cotangents[0], task_weights[0])


def solution(mesh):
    split = Mesh(mesh.devices.reshape(XL, Y, Z, XH, C), AXES)
    task, shard = ("xl", "y"), ("z", "xh", "c")
    in_specs = (
        P(task, shard, None),
        P(task, shard, None),
        P(task, None, shard),
        P(task),
        P(task, None),
        P(task, None),
    )
    return jax.shard_map(
        per_device, mesh=split, in_specs=in_specs, out_specs=P(task, shard), check_vma=False)
```

```python
import jax
import jax.numpy as jnp
from jax import lax
from jax.experimental import pallas as pl
from jax.experimental.pallas import tpu as pltpu
from jax.sharding import Mesh
from jax.sharding import PartitionSpec as P

XL, Y, Z, XH, C = 2, 4, 16, 2, 2
AXES = ("xl", "y", "z", "xh", "c")
EX = 8
MOST = 128
ROWS = 16
CHUNK = 256
NCH = 4
BLK = 256
DB = 512
TILE = 128
HALF = Z // 2
START = (1, 3, 5, 6)
DIRECT = 7
FIRST = 10
PIECES = (1, 1, 1, 1, 1, 1, 1, 1)


def kernel(count_hbm, start_hbm, len_hbm, x_ref, g_ref, w_ref, o_ref,
           xs, gs, ws, fs, fr, mk, count_ref, start_ref, len_ref,
           cr, ov, loc_sem, q_send, q_recv, r_send, r_recv,
           cz_send, cz_recv, gx_send, gx_recv, gc_send, gc_recv,
           w_send, w_recv, f_send, f_recv):
    xl, y, z, xh, c = (lax.axis_index(a) for a in AXES)
    task = xl * Y + y
    oxh, oc = 1 - xh, 1 - c
    quart = c * 2 + xh

    def zmod(v):
        return lax.rem(v + 2 * Z, Z)

    def remote(src, dst, ssem, rsem, **dev):
        return pltpu.make_async_remote_copy(
            src_ref=src, dst_ref=dst, send_sem=ssem, recv_sem=rsem,
            device_id=dev, device_id_type=pl.DeviceIdType.MESH)

    barrier = pltpu.get_barrier_semaphore()

    def tell(**dev):
        pl.semaphore_signal(barrier, inc=1, device_id=dev,
                            device_id_type=pl.DeviceIdType.MESH)

    tell(xh=xh, c=oc)
    tell(xh=oxh, c=c)
    tell(xh=oxh, c=oc)

    tell(z=zmod(z + 1))
    tell(z=zmod(z - 1))

    def tell_t(k, carry):
        t2 = lax.rem(task + k, XL * Y)
        tell(xl=t2 // Y, y=lax.rem(t2, Y))
        return carry
    lax.fori_loop(1, XL * Y, tell_t, 0)

    src_q = task // 2
    src_c, src_xh = src_q // 2, lax.rem(src_q, 2)
    own_src = src_q == quart

    def tell_f(k, carry):
        t2 = lax.rem(task + k, XL * Y)
        tell(xl=t2 // Y, y=lax.rem(t2, Y), xh=src_xh, c=src_c)
        return carry
    lax.fori_loop(1, XL * Y, tell_f, 0)

    @pl.when(jnp.logical_not(own_src))
    def _():
        tell(xh=src_xh, c=src_c)

    me = xh * 2 + c

    def local_x(n):
        return pltpu.make_async_copy(
            x_ref.at[:, pl.ds(pl.multiple_of(quart * 1024 + n * CHUNK, 128), CHUNK)],
            xs.at[n, z, pl.ds(pl.multiple_of(me * ROWS, ROWS), ROWS), :], loc_sem.at[n])

    for n in range(NCH):
        local_x(n).start()
    own_g = g_ref.at[:, pl.ds(pl.multiple_of(z * 1024, 128), 1024)]
    local_g = pltpu.make_async_copy(own_g, gs.at[z, xh, c], loc_sem.at[4])
    local_g.start()
    local_w = pltpu.make_async_copy(
        w_ref.at[pl.ds(pl.multiple_of(task * DB, DB), DB), :], ws.at[task], loc_sem.at[5])
    local_w.start()

    tables = [pltpu.make_async_copy(a, b, loc_sem.at[6 + i]) for i, (a, b) in enumerate(
        ((count_hbm, count_ref), (start_hbm, start_ref), (len_hbm, len_ref)))]
    for copy in tables:
        copy.start()
    for copy in tables:
        copy.wait()

    position = lax.broadcasted_iota(jnp.int32, (MOST, 128), 0)
    for e in range(EX):
        first = start_ref[0, e] - e * MOST
        last = jnp.where(e < count_ref[0], first + len_ref[0, e], first)
        keep = jnp.where(position >= first, 1.0, 0.0) * jnp.where(position < last, 1.0, 0.0)
        mk[e] = keep.astype(jnp.bfloat16)

    pl.semaphore_wait(
        barrier, 3 + 2 + 2 * (XL * Y - 1) + 1 - own_src.astype(jnp.int32))

    def quad_copy(n, h, k):
        return remote(
            x_ref.at[:, pl.ds(pl.multiple_of((k * 2 + h) * 1024 + n * CHUNK, 128), CHUNK)],
            xs.at[n, z, pl.ds(pl.multiple_of(me * ROWS, ROWS), ROWS), :],
            q_send.at[n, h * 2 + k], q_recv.at[n, me], xh=h, c=k)

    def quad_arrival(n, h, k):
        return remote(
            x_ref.at[:, pl.ds(0, CHUNK)],
            xs.at[n, z, pl.ds(pl.multiple_of((h * 2 + k) * ROWS, ROWS), ROWS), :],
            q_send.at[n, me], q_recv.at[n, h * 2 + k], xh=h, c=k)

    others = ((oxh, c), (xh, oc), (oxh, oc))

    def order(m):
        return lax.rem(m + y, 2) * 2 + m // 2

    def cols(way, dist, base):
        width = 512 if dist == HALF else 1024
        off = 512 if dist == HALF and way == 1 else 0
        return pl.ds(pl.multiple_of(base + off, 128), width)

    def cz(way, s, r, src, dst):
        return remote(src, dst, cz_send.at[way, s - 1, r], cz_recv.at[way, s - 1, r],
                      z=zmod(z + (1 if way == 0 else -1)))

    def cz_arrival(way, s, r, far):
        dst = cr.at[way, 0, 0, :, cols(way, HALF if far else 0, 0)]
        cz(way, s, r, dst, dst).wait_recv()

    def cz_first(way, r):
        far = r + 1 == HALF
        dest = zmod(z + (r + 1) * (1 if way == 0 else -1))
        src = g_ref.at[:, cols(way, r + 1, dest * 1024)]
        if r == 0:
            dst = gs.at[z, xh, c]
        else:
            dst = cr.at[way, 0, r - 1, :, cols(way, r + 1, 0)]
        cz(way, 1, r, src, dst).start()

    def cz_pass(way, s, r, far, final):
        cz_arrival(way, s - 1, r + 1, far)
        dist = HALF if far else 0
        src = cr.at[way, s - 2, r, :, cols(way, dist, 0)]
        if final:
            origin = zmod(z - (s - 1) * (1 if way == 0 else -1))
            dst = gs.at[origin, xh, c, :, cols(way, dist, 0)]
        else:
            dst = cr.at[way, s - 1, r - 1, :, cols(way, dist, 0)]
        cz(way, s, r, src, dst).start()

    def cz_step(s):
        @pl.when(s < HALF)
        def _():
            for way in range(2):
                cz_pass(way, s, HALF - s, True, False)

            def middle(j, carry):
                for way in range(2):
                    cz_pass(way, s, HALF - 1 - s - j, False, False)
                return carry
            lax.fori_loop(0, HALF - 1 - s, middle, 0)
            for way in range(2):
                cz_pass(way, s, 0, False, True)

        @pl.when(s == HALF)
        def _():
            for way in range(2):
                cz_pass(way, s, 0, True, True)

    def cz_wait_send(way, s, r, far):
        src = cr.at[way, 0, 0, :, cols(way, HALF if far else 0, 0)]
        cz(way, s, r, src, src).wait_send()

    def w_copy(k, piece=None):
        t2 = lax.rem(task + k, XL * Y)
        if piece is None:
            base, rows, span = t2 * DB, pl.ds(0, DB), DB
        else:
            base, rows, span = t2 * DB + piece * 64, pl.ds(pl.multiple_of(piece * 64, 64), 64), 64
        return remote(
            w_ref.at[pl.ds(pl.multiple_of(base, 64), span), :], ws.at[task, rows, :],
            w_send.at[k], w_recv.at[k], xl=t2 // Y, y=lax.rem(t2, Y))

    def w_some(piece):
        def one(k, carry):
            w_copy(k, piece).start()
            return carry
        lax.fori_loop(1, XL * Y, one, 0)

    def gx_copy(zp, src):
        return remote(src, gs.at[zp, xh, c], gx_send.at[zp], gx_recv.at[zp], xh=oxh)

    def gx_arrival(zp):
        return remote(own_g, gs.at[zp, oxh, c], gx_send.at[zp], gx_recv.at[zp], xh=oxh)

    def gc_copy(zp, h, src):
        return remote(src, gs.at[zp, h, c], gc_send.at[zp, h], gc_recv.at[0], c=oc)

    def gc_all():
        whole = gs.at[:, :, oc]
        pltpu.make_async_copy(whole, whole, gc_recv.at[0]).wait()

    def pass_on(zp):
        gx_copy(zp, gs.at[zp, xh, c]).start()
        gc_copy(zp, xh, gs.at[zp, xh, c]).start()

    def take_z(s):
        @pl.when(s < HALF)
        def _():
            for way in range(2):
                cz_arrival(way, s, 0, False)
                zp = zmod(z - s * (1 if way == 0 else -1))
                pass_on(zp)

                @pl.when(s >= DIRECT)
                def _(zp=zp):
                    diagonal(zp)

        @pl.when(s == HALF)
        def _():
            for way in range(2):
                cz_arrival(way, s, 0, True)
            pass_on(zmod(z + HALF))
            diagonal(zmod(z + HALF))

    def take_x(zp):
        gx_arrival(zp).wait_recv()
        gc_copy(zp, oxh, gs.at[zp, oxh, c]).start()

    def take_x_last(zp):
        gx_arrival(zp).wait_recv()

    def diagonal(zp):
        block = gs.at[zp, xh, c]
        remote(block, block, gc_send.at[zp, oxh], gc_recv.at[0], xh=oxh, c=oc).start()

    for r in range(HALF - 1, -1, -1):
        for way in range(2):
            cz_first(way, r)

    for m in range(NCH):
        for h, k in others:
            quad_copy(order(m), h, k).start()

    gx_copy(z, own_g).start()
    gc_copy(z, xh, own_g).start()

    def ring(way, s, m):
        n = order(m)
        step = 1 if way == 0 else -1
        held = zmod(z - step * (s - 1))
        return remote(xs.at[n, held], xs.at[n, held], r_send.at[way, m, s - 1],
                      r_recv.at[way, m, s - 1], z=zmod(z + step))

    def ring_arrival(way, s, m):
        n = order(m)
        step = 1 if way == 0 else -1
        came = zmod(z - step * s)
        return remote(xs.at[n, came], xs.at[n, came], r_send.at[way, m, s - 1],
                      r_recv.at[way, m, s - 1], z=zmod(z - step))

    def ring_part(slot, m):
        s = slot - START[m]

        @pl.when(s == 1)
        def _():
            n = order(m)
            local_x(n).wait()
            for h, k in others:
                quad_arrival(n, h, k).wait_recv()

        for way in range(2):
            turns = HALF if (m < 2) == (way == 0) else HALF - 1

            @pl.when(jnp.logical_and(s >= 2, s <= turns + 1))
            def _():
                ring_arrival(way, s - 1, m).wait_recv()

            @pl.when(jnp.logical_and(s >= 1, s <= turns))
            def _():
                ring(way, s, m).start()

    def take_pair(d, fn):
        fn(zmod(z + d))

        @pl.when(d < HALF)
        def _():
            fn(zmod(z - d))

    def early(slot, carry):
        @pl.when(jnp.logical_and(slot >= 2, slot <= HALF))
        def _():
            cz_step(slot)

        @pl.when(slot >= 2)
        def _():
            take_z(slot - 1)

        @pl.when(slot >= 4)
        def _():
            take_pair(slot - 3, take_x)

        @pl.when(slot == 2)
        def _():
            take_x(z)
        for m in range(NCH):
            ring_part(slot, m)
        sent = 0
        for at, n in enumerate(PIECES):
            if n:
                @pl.when(slot == at)
                def _(lo=sent, hi=sent + n):
                    for piece in range(lo, hi):
                        w_some(piece)
            sent += n
        return carry

    for piece in range(PIECES[0]):
        w_some(piece)
    lax.fori_loop(1, FIRST, early, 0)
    take_pair(FIRST - 3, take_x_last)
    take_pair(FIRST - 2, take_x_last)
    local_g.wait()

    gc_all()

    inv = jnp.ones((1, BLK), jnp.float32) / jnp.full((1, BLK), count_ref[0].astype(jnp.float32))

    def tile_of(i):
        b = lax.rem(i // 2 + y, 2)
        return b, (i // 4) * 2 + lax.rem(i, 2)

    def send_part(i, f, act):
        b, r = tile_of(i)
        t2 = quart * 2 + b
        h, k = f // 2, f % 2
        mine = jnp.logical_and(t2 == task, me == f)
        dst = fr.at[task, r]
        src = fs.at[i, f]

        @pl.when(jnp.logical_not(mine))
        def _():
            cp = remote(src, dst, f_send.at[i, f], f_recv.at[task, r],
                        xl=t2 // Y, y=lax.rem(t2, Y), xh=h, c=k)
            if act == "start":
                cp.start()
            else:
                cp.wait_send()

        if act == "start":
            @pl.when(mine)
            def _():
                pltpu.make_async_copy(src, dst, f_recv.at[task, r]).start()

    def compute(i):
        b, r = tile_of(i)
        n = b * 2 + r // 2
        col = pl.multiple_of(lax.rem(r, 2) * TILE, TILE)
        xts = []
        for e in range(EX):
            xe = xs[n, 2 * e:2 * e + 2, :, pl.ds(col, TILE)].reshape(MOST, TILE) * mk[e]
            xts.append(xe.T)
        for f in range(4):
            total = jnp.zeros((TILE, BLK), jnp.float32)
            for e in range(EX):
                ge = gs[2 * e:2 * e + 2, :, :, :, f * BLK:(f + 1) * BLK].reshape(MOST, BLK)
                grad = jnp.dot(xts[e], ge, preferred_element_type=jnp.float32)
                total = total + grad * grad
            fs[i, f] = (total * inv).astype(jnp.bfloat16)
            if f > 0:
                send_part(i, f - 1, "start")

    def tile_step(i, carry):
        for m in range(NCH):
            ring_part(i + FIRST, m)

        @pl.when(i > 0)
        def _():
            send_part(i - 1, 3, "start")
        compute(i)
        return carry
    lax.fori_loop(0, 8, tile_step, 0)
    send_part(7, 3, "start")

    local_w.wait()

    def w_wait(k, carry):
        w_copy(k).wait()
        return carry
    lax.fori_loop(1, XL * Y, w_wait, 0)

    for m in range(NCH):
        for h, k in others:
            quad_copy(order(m), h, k).wait_send()

    def c_out(s, carry):
        for way in range(2):
            cz_wait_send(way, s, HALF - s, True)

        def near(r, carry):
            for way in range(2):
                cz_wait_send(way, s, r, False)
            return carry
        return lax.fori_loop(0, HALF - s, near, carry)
    lax.fori_loop(1, HALF + 1, c_out, 0)

    def q_out(zp, carry):
        gx_copy(zp, own_g).wait_send()
        gc_copy(zp, 0, own_g).wait_send()
        gc_copy(zp, 1, own_g).wait_send()
        return carry
    lax.fori_loop(0, Z, q_out, 0)

    def r_out(s, carry):
        for m in range(NCH):
            for way in range(2):
                ring(way, s, m).wait_send()
        return carry
    lax.fori_loop(1, HALF, r_out, 0)
    for m in range(NCH):
        ring(0 if m < 2 else 1, HALF, m).wait_send()

    def f_out(i, carry):
        for f in range(4):
            send_part(i, f, "wait")
        return carry
    lax.fori_loop(0, 8, f_out, 0)

    def merge(r, carry):
        for t2 in range(XL * Y):
            pltpu.make_async_copy(fs.at[0, 0], fr.at[t2, r], f_recv.at[t2, r]).wait()
        rows = pl.ds(pl.multiple_of(r * TILE, TILE), TILE)
        numer = jnp.zeros((TILE, BLK), jnp.float32)
        denom = jnp.zeros((TILE, BLK), jnp.float32)
        for t2 in range(XL * Y):
            f32 = fr[t2, r].astype(jnp.float32)
            numer = numer + f32 * ws[t2, rows, :].astype(jnp.float32)
            denom = denom + f32
        ov[rows, :] = (numer / (denom + 1e-6)).astype(jnp.bfloat16)
        pltpu.make_async_copy(ov.at[rows, :], o_ref.at[rows, :], loc_sem.at[r]).start()
        return carry
    lax.fori_loop(0, 4, merge, 0)

    def leave(r, carry):
        rows = pl.ds(pl.multiple_of(r * TILE, TILE), TILE)
        pltpu.make_async_copy(ov.at[rows, :], o_ref.at[rows, :], loc_sem.at[r]).wait()
        return carry
    lax.fori_loop(0, 4, leave, 0)


def per_device(acts, cotangents, task_weights, example_count, example_start, example_len):
    dma = pltpu.SemaphoreType.DMA
    vmem = pltpu.VMEM
    bf = jnp.bfloat16
    return pl.pallas_call(
        kernel,
        out_shape=jax.ShapeDtypeStruct((DB, BLK), bf),
        in_specs=[pl.BlockSpec(memory_space=pl.ANY)] * 6,
        out_specs=pl.BlockSpec(memory_space=pl.ANY),
        scratch_shapes=[
            vmem((NCH, Z, 64, CHUNK), bf),
            vmem((Z, 2, 2, ROWS, 1024), bf),
            vmem((8, DB, BLK), bf),
            vmem((8, 4, TILE, BLK), bf),
            vmem((8, 4, TILE, BLK), bf),
            vmem((EX, MOST, 128), bf),
            pltpu.SMEM((1,), jnp.int32), pltpu.SMEM((1, EX), jnp.int32),
            pltpu.SMEM((1, EX), jnp.int32),
            vmem((2, HALF - 1, HALF - 1, ROWS, 1024), bf), vmem((DB, BLK), bf), dma((9,)),
            dma((NCH, 4)), dma((NCH, 4)),
            dma((2, NCH, HALF)), dma((2, NCH, HALF)),
            dma((2, HALF, HALF)), dma((2, HALF, HALF)),
            dma((Z,)), dma((Z,)),
            dma((Z, 2)), dma((1,)),
            dma((8,)), dma((8,)),
            dma((8, 4)), dma((8, 4)),
        ],
        compiler_params=pltpu.CompilerParams(
            collective_id=0, has_side_effects=True, vmem_limit_bytes=67_000_000),
        name="merge",
    )(example_count, example_start, example_len,
      acts[0], cotangents[0], task_weights[0])


def solution(mesh):
    split = Mesh(mesh.devices.reshape(XL, Y, Z, XH, C), AXES)
    task, shard = ("xl", "y"), ("z", "xh", "c")
    in_specs = (
        P(task, shard, None),
        P(task, shard, None),
        P(task, None, shard),
        P(task),
        P(task, None),
        P(task, None),
    )
    return jax.shard_map(
        per_device, mesh=split, in_specs=in_specs, out_specs=P(task, shard), check_vma=False)
```
